128 devices in a mesh: scene: 4 (over y_hi, core), tile: 32 (over y_lo, x, z).
Axes of the slice: x: 4, y: 4 (y_hi: 2, y_lo: 2; y = y_hi * 2 + y_lo), z: 4, core: 2. Of those that a mesh axis runs over, the one named last changes fastest.
Arguments:
- node_latent: bfloat16 [524288, 128], P(('scene', 'tile')), parts along dimension 0, may hold values from -6 to 6
- cotangent: float32 [524288, 128], P(('scene', 'tile')), parts along dimension 0, may hold values from -6 to 6
- neighbours: int32 [12, 524288], P(None, ('scene', 'tile')), parts along dimension 1, may hold values from -1 to 6143, as said below
- send_rows: int32 [128, 2, 1024], P(('scene', 'tile')), parts along dimension 0, may hold values from 0 to 4095
- node_mask: int32 [524288], P(('scene', 'tile')), parts along dimension 0, may hold values 0 or 1
- w_src: bfloat16 [128, 128], replicated, may hold values from -0.5 to 0.5
- w_dst: bfloat16 [128, 128], replicated, may hold values from -0.5 to 0.5
- w_msg: bfloat16 [128, 128], replicated, may hold values from -0.5 to 0.5
- edge_gain: float32 [128], replicated, may hold values from 0.1 to 1.9
- edge_bias: float32 [128], replicated, may hold values from -3 to 3
- w_self: bfloat16 [128, 128], replicated, may hold values from -0.5 to 0.5
- w_agg: bfloat16 [128, 128], replicated, may hold values from -0.5 to 0.5
- node_bias: float32 [128], replicated, may hold values from -3 to 3
- w_out: bfloat16 [128, 128], replicated, may hold values from -0.5 to 0.5
Outputs:
- updated: bfloat16 [524288, 128], P(('scene', 'tile')), parts along dimension 0
- latent_grad: float32 [524288, 128], P(('scene', 'tile')), parts along dimension 0
- grad_src: float32 [512, 128], P('scene'), parts along dimension 0
- grad_dst: float32 [512, 128], P('scene'), parts along dimension 0
- grad_msg: float32 [512, 128], P('scene'), parts along dimension 0
- grad_edge_gain: float32 [512], P('scene'), parts along dimension 0
- grad_edge_bias: float32 [512], P('scene'), parts along dimension 0
- grad_self: float32 [512, 128], P('scene'), parts along dimension 0
- grad_agg: float32 [512, 128], P('scene'), parts along dimension 0
- grad_node_bias: float32 [512], P('scene'), parts along dimension 0
- grad_out: float32 [512, 128], P('scene'), parts along dimension 0
The draws below stay inside these ranges and needn't reach their ends.
There are 4 independent parts, one for each index of `scene`. The reference program is written for one: setup_inputs(seed, part) draws one part's arguments, and reference() takes and returns one part's arrays. A program takes and returns all parts, laid end to end along the dimension named above; an argument that names none is the same for every part. Nothing has to cross between parts.
Inputs may be any that keep to these rules, and one draw needn't show every extreme that they name: `neighbours`: each entry is -1 (empty slot) or a row of the tile's extended list: below 4096 its own nodes, then 1024 rows from the tile below, then 1024 rows from the tile above. `send_rows`: rows of the sending tile's own nodes; a row may appear more than once.
All inputs are finite; a program needn't handle non-finite values. No bound on the sum of `node_mask` on one device may be relied on, other than what follows from the above.
Results may differ from the reference program's by a relative error of at most 0.028.
Values may be sent and summed in bfloat16 or wider, within the bound.
No kernel may reach another device: no remote copies, remote signals or barrier semaphores. Data moves between devices by JAX's collectives and lax.ppermute only.
A program may use at most 448 MiB of HBM per device.

```python
from functools import partial
import jax
import jax.numpy as jnp
from jax import lax

W = 128
DEG = 12
NDEV = 4096
HALO = 1024
TILES = 32
NODES = 131072
N_TILE = 32


def draw_neighbours(key, part):
    shape = (DEG, NODES)
    kinds = jax.random.randint(jax.random.fold_in(key, 11), shape, 0, 20)
    owned = jax.random.randint(jax.random.fold_in(key, 12), shape, 0, NDEV)
    remote = jax.random.randint(jax.random.fold_in(key, 13), shape, NDEV, NDEV + 2 * HALO)
    return jnp.where(kinds < 2, -1, jnp.where(kinds < 5, remote, owned)).astype(jnp.int32)


def set_ends(array, key, low, high):
    index_at = [jax.random.randint(jax.random.fold_in(key, axis), (), 0, length) for axis, length in enumerate(array.shape)]
    longest = array.shape.index(max(array.shape))
    beside = index_at[:longest] + [(index_at[longest] + 1) % array.shape[longest]] + index_at[longest + 1:]
    return array.at[tuple(index_at)].set(low).at[tuple(beside)].set(high)


def level_of(key, extent, cuts, smallest, top_value):
    def one(dim, parts):
        steps = jax.random.uniform(jax.random.fold_in(jax.random.fold_in(key, 6), dim), (parts,), jnp.float32, smallest / len(cuts), top_value / len(cuts))
        return jnp.repeat(jnp.exp(steps), extent[dim] // parts).reshape((-1,) + (1,) * (len(extent) - dim - 1))

    level = one(*cuts[0])
    for cut in cuts[1:]:
        level = level * one(*cut)
    return level


def gaussian(own_key, shape, deviation, bound, split=(), dtype=jnp.bfloat16):
    entries = jax.random.normal(own_key, shape, jnp.float32) * deviation
    if len(split) > 0:
        entries = level_of(own_key, shape, split, -0.22, 0.18) * entries
    return jnp.clip(entries, min=-bound, max=bound).astype(dtype)


def setup_inputs(seed: int = 0, part: int = 0) -> dict:
    streams_of = jax.random.split(jax.random.key(seed), 15)
    part_keys = jax.random.split(jax.random.fold_in(streams_of[14], part), 15)
    node_latent = gaussian(part_keys[0], (NODES, W), 1.0, 6.0, ((0, 32),))
    cotangent = gaussian(part_keys[1], (NODES, W), 1.0, 6.0, ((0, 32),), jnp.float32)
    neighbours = draw_neighbours(jax.random.fold_in(jax.random.fold_in(streams_of[14], part), 71), part)
    send_rows = set_ends(jax.random.randint(part_keys[3], (TILES, 2, HALO), 0, NDEV), jax.random.fold_in(part_keys[3], 1), 0, NDEV - 1).astype(jnp.int32)
    node_mask = set_ends((jax.random.randint(part_keys[4], (NODES,), 0, 4) < 3).astype(jnp.int32), jax.random.fold_in(part_keys[4], 1), 0, 1)
    w_src = gaussian(streams_of[5], (W, W), W ** -0.5, 0.5)
    w_dst = gaussian(streams_of[6], (W, W), W ** -0.5, 0.5)
    w_msg = gaussian(streams_of[7], (W, W), W ** -0.5, 0.5)
    edge_gain = jnp.clip(1.0 + 0.18 * jax.random.normal(streams_of[8], (W,), jnp.float32), 0.1, 1.9)
    edge_bias = gaussian(streams_of[9], (W,), 0.5, 3.0, (), jnp.float32)
    w_self = gaussian(streams_of[10], (W, W), W ** -0.5, 0.5)
    w_agg = gaussian(streams_of[11], (W, W), W ** -0.5, 0.5)
    node_bias = gaussian(streams_of[12], (W,), 0.5, 3.0, (), jnp.float32)
    w_out = gaussian(streams_of[13], (W, W), W ** -0.5, 0.5)
    return dict(node_latent=node_latent, cotangent=cotangent, neighbours=neighbours, send_rows=send_rows, node_mask=node_mask, w_src=w_src, w_dst=w_dst, w_msg=w_msg, edge_gain=edge_gain, edge_bias=edge_bias, w_self=w_self, w_agg=w_agg, node_bias=node_bias, w_out=w_out)


def edge_block(w_msg, edge_gain, proj_src, pieces):
    source, proj_part = pieces
    present = (source >= 0)[:, :, None]
    gathered = proj_src[jnp.maximum(source, 0)] + proj_part[None]
    hidden = jax.nn.silu(gathered).astype(jnp.bfloat16)
    degree, block_rows, feature = hidden.shape
    message = jnp.dot(hidden.reshape(degree * block_rows, feature), w_msg.astype(jnp.bfloat16), preferred_element_type=jnp.float32)
    message = message.reshape(degree, block_rows, feature)
    centre = lax.optimization_barrier(jnp.mean(message, axis=2, keepdims=True))
    spread = lax.optimization_barrier(jnp.mean(jnp.square(message - centre), axis=2, keepdims=True))
    normed = (message - centre) * lax.rsqrt(spread + 1e-05) * edge_gain
    return lax.optimization_barrier(jnp.sum(jnp.where(present, normed, 0.0), axis=0))

def edge_section(eparams, extended32, neighbours, again):
    w_src, w_dst, w_msg, edge_gain, edge_bias = eparams
    degree, node_count = neighbours.shape
    extended = extended32.astype(jnp.bfloat16)
    proj_src = jnp.dot(extended, w_src.astype(jnp.bfloat16), preferred_element_type=jnp.float32)
    proj_dst = jnp.dot(extended[:node_count], w_dst.astype(jnp.bfloat16), preferred_element_type=jnp.float32) + edge_bias
    block_rows = min(node_count, 1024)
    nblocks = node_count // block_rows
    groups = neighbours.reshape(degree, nblocks, block_rows).transpose(1, 0, 2)
    worker = partial(edge_block, w_msg, edge_gain, proj_src)
    if again:
        worker = jax.checkpoint(worker)
    summed = lax.map(worker, (groups, proj_dst.reshape(nblocks, block_rows, -1)))
    return summed.reshape(node_count, -1)

def node_section(nparams, own32, summed_bf, node_mask):
    w_self, w_agg, node_bias, w_out = nparams
    own = own32.astype(jnp.bfloat16)
    inner = jnp.dot(own, w_self.astype(jnp.bfloat16), preferred_element_type=jnp.float32)
    inner = inner + jnp.dot(summed_bf, w_agg.astype(jnp.bfloat16), preferred_element_type=jnp.float32) + node_bias
    update = jax.nn.silu(inner).astype(jnp.bfloat16)
    return own32 + node_mask.astype(jnp.float32)[:, None] * jnp.dot(update, w_out.astype(jnp.bfloat16), preferred_element_type=jnp.float32)

def tile_forward(params, extended32, neighbours, node_mask):
    node_count = neighbours.shape[1]
    summed = edge_section(params[:5], extended32, neighbours, False)
    return node_section(params[5:], extended32[:node_count], summed.astype(jnp.bfloat16), node_mask)

def reference(node_latent, cotangent, neighbours, send_rows, node_mask, w_src, w_dst, w_msg, edge_gain, edge_bias, w_self, w_agg, node_bias, w_out):
    params = tuple((p.astype(jnp.float32) for p in (w_src, w_dst, w_msg, edge_gain, edge_bias, w_self, w_agg, node_bias, w_out)))
    latent32 = node_latent.astype(jnp.float32)
    tiled_nbr = neighbours.reshape(DEG, N_TILE, NDEV).transpose(1, 0, 2)
    tiled_mask = node_mask.reshape(N_TILE, NDEV)

    def scene(params, latent32):
        tiled = latent32.reshape(N_TILE, NDEV, W)
        down_send = jax.vmap(lambda block, listing: block[listing])(tiled, send_rows[:, 0])
        up_send = jax.vmap(lambda block, listing: block[listing])(tiled, send_rows[:, 1])
        extended = jnp.concatenate([tiled, jnp.roll(up_send, 1, axis=0), jnp.roll(down_send, -1, axis=0)], axis=1)

        def one_tile(pieces):
            return tile_forward(params, pieces[0], pieces[1], pieces[2])
        result = lax.map(jax.checkpoint(one_tile), (extended, tiled_nbr, tiled_mask))
        return result.reshape(NODES, W)
    result, backward = jax.vjp(scene, params, latent32)
    grads, latent_grad = backward(cotangent)
    factor = NODES ** (-0.5)
    grads = tuple((g * factor for g in grads))
    return (result.astype(jnp.bfloat16), latent_grad, grads[0], grads[1], grads[2], grads[3], grads[4], grads[5], grads[6], grads[7], grads[8])
```

```python
from functools import partial

import jax
import jax.numpy as jnp
from jax import lax
from jax.experimental import pallas as pl
from jax.experimental.pallas import tpu as pltpu
from jax.sharding import PartitionSpec as P

F32 = jnp.float32
BF16 = jnp.bfloat16
BLOCK = 128
CHAINS = 8
EMPTY = -30000.0
VMEM_LIMIT = 60 << 20


def dot(a, b, ca=1, cb=0):
    return lax.dot_general(a, b, (((ca,), (cb,)), ((), ())), preferred_element_type=F32)


def rows8(value):
    return jnp.sum(value.reshape(value.shape[0] // 8, 8, value.shape[1]), axis=0)


def pick_kernel(send_ref, own_ref, out_ref, table, picked):
    table[...] = own_ref[...].astype(F32)
    step = 128

    def body(i, carry):
        base = pl.multiple_of(i * step, step)
        for j in range(step):
            picked[pl.ds(base + j, 1), :] = table[pl.ds(send_ref[i, j], 1), :]
        return carry

    lax.fori_loop(0, picked.shape[0] // step, body, 0)
    out_ref[...] = picked[...].astype(BF16)


def pick_rows(send_rows, own):
    count = send_rows.size
    return pl.pallas_call(
        pick_kernel,
        in_specs=[
            pl.BlockSpec(memory_space=pltpu.SMEM),
            pl.BlockSpec(memory_space=pltpu.VMEM),
        ],
        out_specs=pl.BlockSpec(memory_space=pltpu.VMEM),
        out_shape=jax.ShapeDtypeStruct((count, own.shape[1]), BF16),
        scratch_shapes=[pltpu.VMEM(own.shape, F32), pltpu.VMEM((count, own.shape[1]), F32)],
        compiler_params=pltpu.CompilerParams(vmem_limit_bytes=VMEM_LIMIT),
        name="pick_rows",
    )(send_rows.reshape(count // 128, 128), own)


def main_kernel(
    idx_new,
    idx_old,
    mask_ref,
    own_ref,
    below_ref,
    above_ref,
    cot_ref,
    w_src,
    w_dst,
    w_msg,
    gain_ref,
    ebias_ref,
    w_self,
    w_agg,
    nbias_ref,
    w_out,
    upd_ref,
    grad_ref,
    halo_ref,
    packed_ref,
    proj,
    gath,
    hid,
    slope,
    xhat,
    inv,
    prod,
    grad_msg,
    dedge,
    nacc,
    dacc,
    dyc,
    pdst,
    wcen,
    wacc,
    vacc,
    *tables,
):
    step = pl.program_id(0)
    nblocks = pl.num_programs(0) - 2
    nodes, width = own_ref.shape
    rim = below_ref.shape[0]
    degree = idx_new.shape[0]
    ones = jnp.full((width, width), 1.0 / width, BF16)
    chunk = 512

    @pl.when(step == 0)
    def _():
        for src, at in ((own_ref, 0), (below_ref, nodes), (above_ref, nodes + rim)):
            for c in range(0, src.shape[0], chunk):
                proj[pl.ds(at + c, chunk), :] = dot(src[pl.ds(c, chunk), :], w_src[...])
        proj[pl.ds(nodes + 2 * rim, 8), :] = jnp.full((8, width), EMPTY, F32)
        for t in tables:
            t[...] = jnp.zeros_like(t)
        wacc[...] = jnp.zeros_like(wacc)
        vacc[...] = jnp.zeros_like(vacc)
        w = w_msg[...].astype(F32)
        w = w - jnp.mean(w, axis=1, keepdims=True)
        high = w.astype(BF16)
        wcen[pl.ds(0, width), :] = high
        wcen[pl.ds(width, width), :] = (w - high.astype(F32)).astype(BF16)

    half = 64
    piece = 256
    edges = degree * BLOCK

    def gather_row(n):
        gath[pl.ds(n, 1), :] = proj[pl.ds(idx_new[n // BLOCK, n % BLOCK], 1), :]

    def scatter_row(n):
        t = tables[n % CHAINS]
        i = idx_old[n // BLOCK, n % BLOCK]
        t[pl.ds(i, 1), :] = t[pl.ds(i, 1), :] + dedge[pl.ds(n, 1), :]

    def layer(feed):
        at = pl.ds(pl.multiple_of((step - 1) * BLOCK, BLOCK), BLOCK)
        own = own_ref[at, :]
        pdst[...] = dot(own, w_dst[...]) + ebias_ref[...]
        feed(0, 32, 0)
        for e in range(0, edges, half):
            a = gath[pl.ds(e, half), :] + pdst[pl.ds(e % BLOCK, half), :]
            s = 0.5 * jnp.tanh(0.5 * a) + 0.5
            h = a * s
            slope[pl.ds(e, half), :] = s + h * (1.0 - s)
            hid[pl.ds(e, half), :] = h.astype(BF16)
            feed(e + half, 16, 0)
        for e in range(0, edges, piece):
            hb = hid[pl.ds(e, piece), :]
            x = dot(jnp.concatenate([hb, hb], axis=1), wcen[...])
            xhat[pl.ds(e, piece), :] = x
            prod[pl.ds(e, piece), :] = (x * x).astype(BF16)
            feed(edges, 32, 40)
        for e in range(0, edges, piece):
            r = lax.rsqrt(dot(prod[pl.ds(e, piece), :], ones) + 1e-05)
            xh = xhat[pl.ds(e, piece), :] * r
            inv[pl.ds(e, piece), :] = r
            xhat[pl.ds(e, piece), :] = xh
            nacc[...] = jnp.sum(xh.reshape(piece // BLOCK, BLOCK, width), axis=0) + (
                nacc[...] if e else 0.0
            )
            feed(edges, 48, 60)
        gain = gain_ref[...]
        total = nacc[...]
        sb = (total * gain).astype(BF16)
        pre = dot(own, w_self[...]) + dot(sb, w_agg[...]) + nbias_ref[...]
        feed(edges, 60, 60)
        row = lax.broadcasted_iota(jnp.int32, (128, 128), 0)
        col = lax.broadcasted_iota(jnp.int32, (128, 128), 1)
        full = jnp.ones((128, 128), BF16)
        m = mask_ref[0].astype(F32)
        mask = dot(jnp.where(row == col, m, 0.0).astype(BF16), full)
        cot = cot_ref[...]
        dob = (cot * mask).astype(BF16)
        du = dot(dob, w_out[...], 1, 1)
        feed(edges, 60, 60)
        s = 0.5 * jnp.tanh(0.5 * pre) + 0.5
        u = pre * s
        dpre = du * (s + u * (1.0 - s))
        ub = u.astype(BF16)
        dpb = dpre.astype(BF16)
        ds = dot(dpb, w_agg[...], 1, 1)
        feed(edges, 60, 60)
        dy = ds * gain
        dyc[...] = dy - jnp.mean(dy, axis=1, keepdims=True)
        feed(edges, 60, 60)
        upd_ref[...] = (own.astype(F32) + mask * dot(ub, w_out[...])).astype(BF16)
        grad_ref[at, :] = cot + dot(dpb, w_self[...], 1, 1)
        wacc[3] += dot(own, dpb, 0, 0)
        wacc[4] += dot(sb, dpb, 0, 0)
        wacc[5] += dot(ub, dob, 0, 0)
        vacc[0] += rows8(ds * total)
        vacc[2] += rows8(dpre)
        feed(edges, 60, 60)
        for e in range(0, edges, half):
            xh = xhat[pl.ds(e, half), :]
            prod[pl.ds(e, half), :] = (dyc[pl.ds(e % BLOCK, half), :] * xh).astype(BF16)
            feed(edges, 8, 8)
        dy = jnp.broadcast_to(dyc[...][None], (piece // BLOCK, BLOCK, width)).reshape(piece, width)
        for e in range(0, edges, piece):
            along = dot(prod[pl.ds(e, piece), :], ones)
            dm = inv[pl.ds(e, piece), :] * (dy - xhat[pl.ds(e, piece), :] * along)
            grad_msg[pl.ds(e, piece), :] = dm.astype(BF16)
            feed(edges, 60, 60)
        feed(edges, edges, 0)
        for e in range(0, edges, piece):
            dh = dot(grad_msg[pl.ds(e, piece), :], w_msg[...], 1, 1)
            da = dh * slope[pl.ds(e, piece), :]
            dedge[pl.ds(e, piece), :] = da
            dacc[...] = jnp.sum(da.reshape(piece // BLOCK, BLOCK, width), axis=0) + (
                dacc[...] if e else 0.0
            )
            feed(edges, 0, 60)
        wacc[2] += dot(hid[...], grad_msg[...], 0, 0)
        d = dacc[...]
        db = d.astype(BF16)
        grad_ref[at, :] += dot(db, w_dst[...], 1, 1)
        wacc[1] += dot(own, db, 0, 0)
        vacc[1] += rows8(d)
        feed(edges, edges, edges)

    @pl.when(step == 0)
    def _():
        dedge[...] = jnp.zeros_like(dedge)
        for n in range(edges):
            gather_row(n)

    @pl.when((step > 0) & (step <= nblocks))
    def _():
        done = [0, 0]

        def feed(ready, scatters, gathers):
            while scatters > 0 or gathers > 0:
                if scatters > 0 and done[0] < edges:
                    scatter_row(done[0])
                    done[0] += 1
                if gathers > 0 and done[1] < ready:
                    gather_row(done[1])
                    done[1] += 1
                scatters -= 1
                gathers -= 1

        layer(feed)

    @pl.when(step == nblocks + 1)
    def _():
        for n in range(edges):
            scatter_row(n)

    @pl.when(step == nblocks + 1)
    def _():
        gsrc = jnp.zeros((width, width), F32)
        for src, at in ((own_ref, 0), (below_ref, nodes), (above_ref, nodes + rim)):
            for c in range(0, src.shape[0], chunk):
                d = tables[0][pl.ds(at + c, chunk), :]
                for t in tables[1:]:
                    d = d + t[pl.ds(at + c, chunk), :]
                db = d.astype(BF16)
                back = dot(db, w_src[...], 1, 1)
                if at == 0:
                    grad_ref[pl.ds(c, chunk), :] += back
                else:
                    halo_ref[pl.ds(at - nodes + c, chunk), :] = back.astype(BF16)
                gsrc = gsrc + dot(src[pl.ds(c, chunk), :], db, 0, 0)
        wacc[0] = gsrc
        for n in range(6):
            packed_ref[pl.ds(n * width, width), :] = wacc[n].astype(BF16)
        pick = lax.broadcasted_iota(jnp.int32, (16, width), 0)
        tail = jnp.zeros((16, width), F32)
        for n in range(3):
            tail = jnp.where(pick == n, jnp.sum(vacc[n], axis=0, keepdims=True), tail)
        packed_ref[pl.ds(6 * width, 16), :] = tail.astype(BF16)
        rest = packed_ref.shape[0] - 6 * width - 16
        packed_ref[pl.ds(6 * width + 16, rest), :] = jnp.zeros((rest, width), BF16)


def main_call(own, below, above, cotangent, idx, mask, weights):
    nodes, width = own.shape
    rim = below.shape[0]
    degree = idx.shape[0]
    nblocks = nodes // BLOCK
    table = nodes + 2 * rim + 8
    whole = pl.BlockSpec(memory_space=pltpu.VMEM)

    def now(i):
        return jnp.minimum(i, nblocks - 1)

    def held(i):
        return jnp.clip(i - 1, 0, nblocks - 1)

    def before(i):
        return jnp.maximum(i - 2, 0)

    w_src, w_dst, w_msg, gain, ebias, w_self, w_agg, nbias, w_out = weights
    edges = degree * BLOCK
    fixed = lambda shape: pl.BlockSpec(shape, lambda i: (0,) * len(shape))
    scratch = [
        pltpu.VMEM((table, width), F32),
        pltpu.VMEM((edges, width), F32),
        pltpu.VMEM((edges, width), BF16),
        pltpu.VMEM((edges, width), F32),
        pltpu.VMEM((edges, width), F32),
        pltpu.VMEM((edges, width), F32),
        pltpu.VMEM((edges, width), BF16),
        pltpu.VMEM((edges, width), BF16),
        pltpu.VMEM((edges, width), F32),
        pltpu.VMEM((BLOCK, width), F32),
        pltpu.VMEM((BLOCK, width), F32),
        pltpu.VMEM((BLOCK, width), F32),
        pltpu.VMEM((BLOCK, width), F32),
        pltpu.VMEM((2 * width, width), BF16),
        pltpu.VMEM((6, width, width), F32),
        pltpu.VMEM((3, 8, width), F32),
    ] + [pltpu.VMEM((table, width), F32) for _ in range(CHAINS)]
    return pl.pallas_call(
        main_kernel,
        grid=(nblocks + 2,),
        in_specs=[
            pl.BlockSpec((degree, BLOCK), lambda i: (0, now(i)), memory_space=pltpu.SMEM),
            pl.BlockSpec((degree, BLOCK), lambda i: (0, before(i)), memory_space=pltpu.SMEM),
            pl.BlockSpec((BLOCK // 128, 1, 128), lambda i: (held(i), 0, 0)),
            fixed(own.shape),
            fixed(below.shape),
            fixed(above.shape),
            pl.BlockSpec((BLOCK, width), lambda i: (held(i), 0)),
        ]
        + [fixed((width, width))] * 3
        + [fixed((1, width))] * 2
        + [fixed((width, width))] * 2
        + [fixed((1, width))]
        + [fixed((width, width))],
        out_specs=[
            pl.BlockSpec((BLOCK, width), lambda i: (held(i), 0)),
            fixed((nodes, width)),
            fixed((2 * rim, width)),
            fixed((8 * width, width)),
        ],
        out_shape=[
            jax.ShapeDtypeStruct((nodes, width), BF16),
            jax.ShapeDtypeStruct((nodes, width), F32),
            jax.ShapeDtypeStruct((2 * rim, width), BF16),
            jax.ShapeDtypeStruct((8 * width, width), BF16),
        ],
        scratch_shapes=scratch,
        compiler_params=pltpu.CompilerParams(
            dimension_semantics=("arbitrary",), vmem_limit_bytes=VMEM_LIMIT
        ),
        name="main_layer",
    )(
        idx,
        idx,
        mask,
        own,
        below,
        above,
        cotangent,
        w_src,
        w_dst,
        w_msg,
        gain.reshape(1, width),
        ebias.reshape(1, width),
        w_self,
        w_agg,
        nbias.reshape(1, width),
        w_out,
    )


def add_kernel(send_ref, part_ref, first_ref, second_ref, out_ref, back, *tables):
    rim = first_ref.shape[0]
    back[pl.ds(0, rim), :] = first_ref[...].astype(F32)
    back[pl.ds(rim, rim), :] = second_ref[...].astype(F32)
    for t in tables:
        t[...] = jnp.zeros_like(t)
    step = 128

    def body(i, carry):
        base = pl.multiple_of(i * step, step)
        for j in range(step):
            t = tables[j % len(tables)]
            at = pl.ds(send_ref[i, j], 1)
            t[at, :] = t[at, :] + back[pl.ds(base + j, 1), :]
        return carry

    lax.fori_loop(0, 2 * rim // step, body, 0)
    total = part_ref[...]
    for t in tables:
        total = total + t[...]
    out_ref[...] = total


def add_returned(send_rows, part, first, second):
    nodes, width = part.shape
    rim = first.shape[0]
    vmem = pl.BlockSpec(memory_space=pltpu.VMEM)
    return pl.pallas_call(
        add_kernel,
        in_specs=[pl.BlockSpec(memory_space=pltpu.SMEM), vmem, vmem, vmem],
        out_specs=vmem,
        out_shape=jax.ShapeDtypeStruct(part.shape, F32),
        scratch_shapes=[pltpu.VMEM((2 * rim, width), F32)]
        + [pltpu.VMEM((nodes, width), F32) for _ in range(CHAINS)],
        compiler_params=pltpu.CompilerParams(vmem_limit_bytes=VMEM_LIMIT),
        input_output_aliases={1: 0},
        name="add_returned",
    )(send_rows.reshape(2 * rim // 128, 128), part, first, second)


def sum_kernel(parts_ref, out_ref):
    total = parts_ref[0].astype(F32)
    for n in range(1, parts_ref.shape[0]):
        total = total + parts_ref[n].astype(F32)
    out_ref[...] = jnp.broadcast_to(total.astype(BF16)[None], out_ref.shape)


def finish_kernel(factor, sums_ref, *outs):
    width = sums_ref.shape[1]
    for n in range(6):
        outs[n][...] = sums_ref[pl.ds(n * width, width), :].astype(F32) * factor
    tail = sums_ref[pl.ds(6 * width, 16), :].astype(F32) * factor
    for n in range(3):
        outs[6 + n][...] = tail[n : n + 1, :]


def weight_sums(packed, factor):
    size = lax.axis_size("tile")
    count, width = packed.shape
    share = count // size
    vmem = pl.BlockSpec(memory_space=pltpu.VMEM)
    parts = lax.all_to_all(packed.reshape(size, share, width), "tile", 0, 0, tiled=True)
    mine = pl.pallas_call(
        sum_kernel,
        in_specs=[vmem],
        out_specs=vmem,
        out_shape=jax.ShapeDtypeStruct((size, share, width), BF16),
        name="sum_parts",
    )(parts)
    sums = lax.all_to_all(mine, "tile", 0, 0, tiled=True).reshape(count, width)
    outs = pl.pallas_call(
        partial(finish_kernel, factor),
        in_specs=[vmem],
        out_specs=[vmem] * 9,
        out_shape=[jax.ShapeDtypeStruct((width, width), F32)] * 6
        + [jax.ShapeDtypeStruct((1, width), F32)] * 3,
        name="finish_weights",
    )(sums)
    return outs[:6], [v.reshape(width) for v in outs[6:]]


def on_device(
    node_latent,
    cotangent,
    neighbours,
    send_rows,
    node_mask,
    w_src,
    w_dst,
    w_msg,
    edge_gain,
    edge_bias,
    w_self,
    w_agg,
    node_bias,
    w_out,
):
    nodes = node_latent.shape[0]
    rim = send_rows.shape[2]
    size = lax.axis_size("tile")
    up = [(i, (i + 1) % size) for i in range(size)]
    down = [(j, i) for i, j in up]
    send = send_rows[0]
    outbound = pick_rows(send, node_latent)
    below = lax.ppermute(outbound[rim:], "tile", up)
    above = lax.ppermute(outbound[:rim], "tile", down)
    idx = jnp.where(neighbours < 0, nodes + 2 * rim, neighbours)
    mask = node_mask.reshape(nodes // 128, 1, 128)
    weights = (w_src, w_dst, w_msg, edge_gain, edge_bias, w_self, w_agg, node_bias, w_out)
    updated, part, halo, packed = main_call(
        node_latent, below, above, cotangent, idx, mask, weights
    )
    first = lax.ppermute(halo[rim:], "tile", up)
    second = lax.ppermute(halo[:rim], "tile", down)
    latent_grad = add_returned(send, part, first, second)
    factor = (nodes * size) ** (-0.5)
    mats, vecs = weight_sums(packed, factor)
    g_src, g_dst, g_msg, g_self, g_agg, g_out = mats
    g_gain, g_ebias, g_nbias = vecs
    return (
        updated,
        latent_grad,
        g_src,
        g_dst,
        g_msg,
        g_gain,
        g_ebias,
        g_self,
        g_agg,
        g_nbias,
        g_out,
    )


def solution(mesh):
    tiles = ("scene", "tile")
    in_specs = (
        P(tiles, None),
        P(tiles, None),
        P(None, tiles),
        P(tiles, None, None),
        P(tiles),
    ) + (P(),) * 9
    mat, vec = P("scene", None), P("scene")
    out_specs = (P(tiles, None), P(tiles, None), mat, mat, mat, vec, vec, mat, mat, vec, mat)
    return jax.shard_map(
        on_device, mesh=mesh, in_specs=in_specs, out_specs=out_specs, check_vma=False
    )
```

```python
from functools import partial

import jax
import jax.numpy as jnp
from jax import lax
from jax.experimental import pallas as pl
from jax.experimental.pallas import tpu as pltpu
from jax.sharding import PartitionSpec as P

F32 = jnp.float32
BF16 = jnp.bfloat16
BLOCK = 256
CHAINS = 8
EMPTY = -30000.0
VMEM_LIMIT = 60 << 20


def dot(a, b, ca=1, cb=0):
    return lax.dot_general(a, b, (((ca,), (cb,)), ((), ())), preferred_element_type=F32)


def rows8(value):
    return jnp.sum(value.reshape(value.shape[0] // 8, 8, value.shape[1]), axis=0)


def pick_kernel(send_ref, own_ref, down_ref, up_ref, table, picked):
    table[...] = own_ref[...].astype(F32)
    step = 128

    def body(i, carry):
        base = pl.multiple_of(i * step, step)
        for j in range(step):
            picked[pl.ds(base + j, 1), :] = table[pl.ds(send_ref[i, j], 1), :]
        return carry

    lax.fori_loop(0, picked.shape[0] // step, body, 0)
    rim = down_ref.shape[0]
    down_ref[...] = picked[pl.ds(0, rim), :].astype(BF16)
    up_ref[...] = picked[pl.ds(rim, rim), :].astype(BF16)


def pick_rows(send_rows, own):
    count = send_rows.size
    return pl.pallas_call(
        pick_kernel,
        in_specs=[
            pl.BlockSpec(memory_space=pltpu.SMEM),
            pl.BlockSpec(memory_space=pltpu.VMEM),
        ],
        out_specs=[pl.BlockSpec(memory_space=pltpu.VMEM)] * 2,
        out_shape=[jax.ShapeDtypeStruct((count // 2, own.shape[1]), BF16)] * 2,
        scratch_shapes=[pltpu.VMEM(own.shape, F32), pltpu.VMEM((count, own.shape[1]), F32)],
        compiler_params=pltpu.CompilerParams(vmem_limit_bytes=VMEM_LIMIT),
        name="pick_rows",
    )(send_rows.reshape(count // 128, 128), own)


def main_kernel(
    idx_new,
    idx_old,
    mask_ref,
    own_ref,
    below_ref,
    above_ref,
    cot_ref,
    w_src,
    w_dst,
    w_msg,
    gain_ref,
    ebias_ref,
    w_self,
    w_agg,
    nbias_ref,
    w_out,
    upd_ref,
    grad_ref,
    back_below_ref,
    back_above_ref,
    packed_ref,
    proj,
    gath,
    hid,
    slope,
    xhat,
    inv,
    prod,
    grad_msg,
    dedge,
    nacc,
    dacc,
    dyc,
    pdst,
    wcen,
    wacc,
    vacc,
    *tables,
):
    step = pl.program_id(0)
    nblocks = pl.num_programs(0) - 1
    nodes, width = own_ref.shape
    rim = below_ref.shape[0]
    degree = idx_new.shape[0]
    ones = jnp.full((width, width), 1.0 / width, BF16)
    chunk = 512

    @pl.when(step == 0)
    def _():
        for src, at in ((own_ref, 0), (below_ref, nodes), (above_ref, nodes + rim)):
            for c in range(0, src.shape[0], chunk):
                proj[pl.ds(at + c, chunk), :] = dot(src[pl.ds(c, chunk), :], w_src[...])
        proj[pl.ds(nodes + 2 * rim, 8), :] = jnp.full((8, width), EMPTY, F32)
        for t in tables:
            t[...] = jnp.zeros_like(t)
        wacc[...] = jnp.zeros_like(wacc)
        vacc[...] = jnp.zeros_like(vacc)
        w = w_msg[...].astype(F32)
        w = w - jnp.mean(w, axis=1, keepdims=True)
        high = w.astype(BF16)
        wcen[pl.ds(0, width), :] = high
        wcen[pl.ds(width, width), :] = (w - high.astype(F32)).astype(BF16)

    half = 64
    piece = 256
    edges = degree * BLOCK

    def gather_row(n):
        gath[pl.ds(n, 1), :] = proj[pl.ds(idx_new[n // BLOCK, n % BLOCK], 1), :]

    def scatter_row(n):
        t = tables[n % CHAINS]
        i = idx_old[n // BLOCK, n % BLOCK]
        t[pl.ds(i, 1), :] = t[pl.ds(i, 1), :] + dedge[pl.ds(n, 1), :]

    def layer():
        at = pl.ds(pl.multiple_of((step - 1) * BLOCK, BLOCK), BLOCK)
        own = own_ref[at, :]
        pdst[...] = dot(own, w_dst[...]) + ebias_ref[...]
        for e in range(0, edges, half):
            a = gath[pl.ds(e, half), :] + pdst[pl.ds(e % BLOCK, half), :]
            s = 0.5 * jnp.tanh(0.5 * a) + 0.5
            h = a * s
            slope[pl.ds(e, half), :] = s + h * (1.0 - s)
            hid[pl.ds(e, half), :] = h.astype(BF16)
        for e in range(0, edges, piece):
            hb = hid[pl.ds(e, piece), :]
            x = dot(jnp.concatenate([hb, hb], axis=1), wcen[...])
            xhat[pl.ds(e, piece), :] = x
            prod[pl.ds(e, piece), :] = (x * x).astype(BF16)
        for e in range(0, edges, piece):
            r = lax.rsqrt(dot(prod[pl.ds(e, piece), :], ones) + 1e-05)
            xh = xhat[pl.ds(e, piece), :] * r
            inv[pl.ds(e, piece), :] = r
            xhat[pl.ds(e, piece), :] = xh
            nacc[...] = jnp.sum(xh.reshape(piece // BLOCK, BLOCK, width), axis=0) + (
                nacc[...] if e else 0.0
            )
        gain = gain_ref[...]
        total = nacc[...]
        sb = (total * gain).astype(BF16)
        pre = dot(own, w_self[...]) + dot(sb, w_agg[...]) + nbias_ref[...]
        row = lax.broadcasted_iota(jnp.int32, (128, 128), 0)
        col = lax.broadcasted_iota(jnp.int32, (128, 128), 1)
        full = jnp.ones((128, 128), BF16)
        mask = []
        for n in range(BLOCK // 128):
            m = mask_ref[n].astype(F32)
            mask.append(dot(jnp.where(row == col, m, 0.0).astype(BF16), full))
        mask = jnp.concatenate(mask, axis=0)
        cot = cot_ref[...]
        dob = (cot * mask).astype(BF16)
        du = dot(dob, w_out[...], 1, 1)
        s = 0.5 * jnp.tanh(0.5 * pre) + 0.5
        u = pre * s
        dpre = du * (s + u * (1.0 - s))
        ub = u.astype(BF16)
        dpb = dpre.astype(BF16)
        ds = dot(dpb, w_agg[...], 1, 1)
        dy = ds * gain
        dyc[...] = dy - jnp.mean(dy, axis=1, keepdims=True)
        upd_ref[...] = (own.astype(F32) + mask * dot(ub, w_out[...])).astype(BF16)
        grad_ref[at, :] = cot + dot(dpb, w_self[...], 1, 1)
        wacc[3] += dot(own, dpb, 0, 0)
        wacc[4] += dot(sb, dpb, 0, 0)
        wacc[5] += dot(ub, dob, 0, 0)
        vacc[0] += rows8(ds * total)
        vacc[2] += rows8(dpre)
        for e in range(0, edges, half):
            xh = xhat[pl.ds(e, half), :]
            prod[pl.ds(e, half), :] = (dyc[pl.ds(e % BLOCK, half), :] * xh).astype(BF16)
        dy = jnp.broadcast_to(dyc[...][None], (piece // BLOCK, BLOCK, width)).reshape(piece, width)
        for e in range(0, edges, piece):
            along = dot(prod[pl.ds(e, piece), :], ones)
            dm = inv[pl.ds(e, piece), :] * (dy - xhat[pl.ds(e, piece), :] * along)
            grad_msg[pl.ds(e, piece), :] = dm.astype(BF16)
        for e in range(0, edges, piece):
            dh = dot(grad_msg[pl.ds(e, piece), :], w_msg[...], 1, 1)
            da = dh * slope[pl.ds(e, piece), :]
            dedge[pl.ds(e, piece), :] = da
            dacc[...] = jnp.sum(da.reshape(piece // BLOCK, BLOCK, width), axis=0) + (
                dacc[...] if e else 0.0
            )
        wacc[2] += dot(hid[...], grad_msg[...], 0, 0)
        d = dacc[...]
        db = d.astype(BF16)
        grad_ref[at, :] += dot(db, w_dst[...], 1, 1)
        wacc[1] += dot(own, db, 0, 0)
        vacc[1] += rows8(d)

    @pl.when(step == 0)
    def _():
        for n in range(edges):
            gather_row(n)

    @pl.when(step > 0)
    def _():
        layer()
        for n in range(edges):
            scatter_row(n)
            gather_row(n)

    @pl.when(step == nblocks)
    def _():
        gsrc = jnp.zeros((width, width), F32)
        for src, at, out_ref in (
            (own_ref, 0, None),
            (below_ref, nodes, back_below_ref),
            (above_ref, nodes + rim, back_above_ref),
        ):
            for c in range(0, src.shape[0], chunk):
                d = tables[0][pl.ds(at + c, chunk), :]
                for t in tables[1:]:
                    d = d + t[pl.ds(at + c, chunk), :]
                db = d.astype(BF16)
                back = dot(db, w_src[...], 1, 1)
                if out_ref is None:
                    grad_ref[pl.ds(c, chunk), :] += back
                else:
                    out_ref[pl.ds(c, chunk), :] = back.astype(BF16)
                gsrc = gsrc + dot(src[pl.ds(c, chunk), :], db, 0, 0)
        wacc[0] = gsrc
        for n in range(6):
            packed_ref[pl.ds(n * width, width), :] = wacc[n].astype(BF16)
        pick = lax.broadcasted_iota(jnp.int32, (16, width), 0)
        tail = jnp.zeros((16, width), F32)
        for n in range(3):
            tail = jnp.where(pick == n, jnp.sum(vacc[n], axis=0, keepdims=True), tail)
        packed_ref[pl.ds(6 * width, 16), :] = tail.astype(BF16)
        rest = packed_ref.shape[0] - 6 * width - 16
        packed_ref[pl.ds(6 * width + 16, rest), :] = jnp.zeros((rest, width), BF16)


def main_call(own, below, above, cotangent, idx, mask, weights):
    nodes, width = own.shape
    rim = below.shape[0]
    degree = idx.shape[0]
    nblocks = nodes // BLOCK
    table = nodes + 2 * rim + 8
    whole = pl.BlockSpec(memory_space=pltpu.VMEM)

    def now(i):
        return jnp.minimum(i, nblocks - 1)

    def held(i):
        return jnp.clip(i - 1, 0, nblocks - 1)


    w_src, w_dst, w_msg, gain, ebias, w_self, w_agg, nbias, w_out = weights
    edges = degree * BLOCK
    fixed = lambda shape: pl.BlockSpec(shape, lambda i: (0,) * len(shape))
    scratch = [
        pltpu.VMEM((table, width), F32),
        pltpu.VMEM((edges, width), F32),
        pltpu.VMEM((edges, width), BF16),
        pltpu.VMEM((edges, width), F32),
        pltpu.VMEM((edges, width), F32),
        pltpu.VMEM((edges, width), F32),
        pltpu.VMEM((edges, width), BF16),
        pltpu.VMEM((edges, width), BF16),
        pltpu.VMEM((edges, width), F32),
        pltpu.VMEM((BLOCK, width), F32),
        pltpu.VMEM((BLOCK, width), F32),
        pltpu.VMEM((BLOCK, width), F32),
        pltpu.VMEM((BLOCK, width), F32),
        pltpu.VMEM((2 * width, width), BF16),
        pltpu.VMEM((6, width, width), F32),
        pltpu.VMEM((3, 8, width), F32),
    ] + [pltpu.VMEM((table, width), F32) for _ in range(CHAINS)]
    return pl.pallas_call(
        main_kernel,
        grid=(nblocks + 1,),
        in_specs=[
            pl.BlockSpec((degree, BLOCK), lambda i: (0, now(i)), memory_space=pltpu.SMEM),
            pl.BlockSpec((degree, BLOCK), lambda i: (0, held(i)), memory_space=pltpu.SMEM),
            pl.BlockSpec((BLOCK // 128, 1, 128), lambda i: (held(i), 0, 0)),
            fixed(own.shape),
            fixed(below.shape),
            fixed(above.shape),
            pl.BlockSpec((BLOCK, width), lambda i: (held(i), 0)),
        ]
        + [fixed((width, width))] * 3
        + [fixed((1, width))] * 2
        + [fixed((width, width))] * 2
        + [fixed((1, width))]
        + [fixed((width, width))],
        out_specs=[
            pl.BlockSpec((BLOCK, width), lambda i: (held(i), 0)),
            fixed((nodes, width)),
            fixed((rim, width)),
            fixed((rim, width)),
            fixed((8 * width, width)),
        ],
        out_shape=[
            jax.ShapeDtypeStruct((nodes, width), BF16),
            jax.ShapeDtypeStruct((nodes, width), F32),
            jax.ShapeDtypeStruct((rim, width), BF16),
            jax.ShapeDtypeStruct((rim, width), BF16),
            jax.ShapeDtypeStruct((8 * width, width), BF16),
        ],
        scratch_shapes=scratch,
        compiler_params=pltpu.CompilerParams(
            dimension_semantics=("arbitrary",), vmem_limit_bytes=VMEM_LIMIT
        ),
        name="main_layer",
    )(
        idx,
        idx,
        mask,
        own,
        below,
        above,
        cotangent,
        w_src,
        w_dst,
        w_msg,
        gain.reshape(1, width),
        ebias.reshape(1, width),
        w_self,
        w_agg,
        nbias.reshape(1, width),
        w_out,
    )


def add_kernel(send_ref, part_ref, first_ref, second_ref, out_ref, back, *tables):
    rim = first_ref.shape[0]
    back[pl.ds(0, rim), :] = first_ref[...].astype(F32)
    back[pl.ds(rim, rim), :] = second_ref[...].astype(F32)
    for t in tables:
        t[...] = jnp.zeros_like(t)
    step = 128

    def body(i, carry):
        base = pl.multiple_of(i * step, step)
        for j in range(step):
            t = tables[j % len(tables)]
            at = pl.ds(send_ref[i, j], 1)
            t[at, :] = t[at, :] + back[pl.ds(base + j, 1), :]
        return carry

    lax.fori_loop(0, 2 * rim // step, body, 0)
    total = part_ref[...]
    for t in tables:
        total = total + t[...]
    out_ref[...] = total


def add_returned(send_rows, part, first, second):
    nodes, width = part.shape
    rim = first.shape[0]
    vmem = pl.BlockSpec(memory_space=pltpu.VMEM)
    return pl.pallas_call(
        add_kernel,
        in_specs=[pl.BlockSpec(memory_space=pltpu.SMEM), vmem, vmem, vmem],
        out_specs=vmem,
        out_shape=jax.ShapeDtypeStruct(part.shape, F32),
        scratch_shapes=[pltpu.VMEM((2 * rim, width), F32)]
        + [pltpu.VMEM((nodes, width), F32) for _ in range(CHAINS)],
        compiler_params=pltpu.CompilerParams(vmem_limit_bytes=VMEM_LIMIT),
        input_output_aliases={1: 0},
        name="add_returned",
    )(send_rows.reshape(2 * rim // 128, 128), part, first, second)


def sum_kernel(parts_ref, out_ref):
    total = parts_ref[0].astype(F32)
    for n in range(1, parts_ref.shape[0]):
        total = total + parts_ref[n].astype(F32)
    out_ref[...] = jnp.broadcast_to(total.astype(BF16)[None], out_ref.shape)


def finish_kernel(factor, sums_ref, *outs):
    width = sums_ref.shape[1]
    for n in range(6):
        outs[n][...] = sums_ref[pl.ds(n * width, width), :].astype(F32) * factor
    tail = sums_ref[pl.ds(6 * width, 16), :].astype(F32) * factor
    for n in range(3):
        outs[6 + n][...] = tail[n : n + 1, :]


def weight_sums(packed, factor):
    size = lax.axis_size("tile")
    count, width = packed.shape
    share = count // size
    vmem = pl.BlockSpec(memory_space=pltpu.VMEM)
    parts = lax.all_to_all(packed.reshape(size, share, width), "tile", 0, 0, tiled=True)
    mine = pl.pallas_call(
        sum_kernel,
        in_specs=[vmem],
        out_specs=vmem,
        out_shape=jax.ShapeDtypeStruct((size, share, width), BF16),
        name="sum_parts",
    )(parts)
    sums = lax.all_to_all(mine, "tile", 0, 0, tiled=True).reshape(count, width)
    outs = pl.pallas_call(
        partial(finish_kernel, factor),
        in_specs=[vmem],
        out_specs=[vmem] * 9,
        out_shape=[jax.ShapeDtypeStruct((width, width), F32)] * 6
        + [jax.ShapeDtypeStruct((1, width), F32)] * 3,
        name="finish_weights",
    )(sums)
    return outs[:6], [v.reshape(width) for v in outs[6:]]


def on_device(
    node_latent,
    cotangent,
    neighbours,
    send_rows,
    node_mask,
    w_src,
    w_dst,
    w_msg,
    edge_gain,
    edge_bias,
    w_self,
    w_agg,
    node_bias,
    w_out,
):
    nodes = node_latent.shape[0]
    rim = send_rows.shape[2]
    size = lax.axis_size("tile")
    up = [(i, (i + 1) % size) for i in range(size)]
    down = [(j, i) for i, j in up]
    send = send_rows[0]
    to_below, to_above = pick_rows(send, node_latent)
    below = lax.ppermute(to_above, "tile", up)
    above = lax.ppermute(to_below, "tile", down)
    idx = jnp.where(neighbours < 0, nodes + 2 * rim, neighbours)
    mask = node_mask.reshape(nodes // 128, 1, 128)
    weights = (w_src, w_dst, w_msg, edge_gain, edge_bias, w_self, w_agg, node_bias, w_out)
    updated, part, back_below, back_above, packed = main_call(
        node_latent, below, above, cotangent, idx, mask, weights
    )
    first = lax.ppermute(back_above, "tile", up)
    second = lax.ppermute(back_below, "tile", down)
    latent_grad = add_returned(send, part, first, second)
    factor = (nodes * size) ** (-0.5)
    mats, vecs = weight_sums(packed, factor)
    g_src, g_dst, g_msg, g_self, g_agg, g_out = mats
    g_gain, g_ebias, g_nbias = vecs
    return (
        updated,
        latent_grad,
        g_src,
        g_dst,
        g_msg,
        g_gain,
        g_ebias,
        g_self,
        g_agg,
        g_nbias,
        g_out,
    )


def solution(mesh):
    tiles = ("scene", "tile")
    in_specs = (
        P(tiles, None),
        P(tiles, None),
        P(None, tiles),
        P(tiles, None, None),
        P(tiles),
    ) + (P(),) * 9
    mat, vec = P("scene", None), P("scene")
    out_specs = (P(tiles, None), P(tiles, None), mat, mat, mat, vec, vec, mat, mat, vec, mat)
    return jax.shard_map(
        on_device, mesh=mesh, in_specs=in_specs, out_specs=out_specs, check_vma=False
    )
```

```python
from functools import partial

import jax
import jax.numpy as jnp
from jax import lax
from jax.experimental import pallas as pl
from jax.experimental.pallas import tpu as pltpu
from jax.sharding import PartitionSpec as P

F32 = jnp.float32
BF16 = jnp.bfloat16
BLOCK = 256
CHAINS = 8
EMPTY = -30000.0
VMEM_LIMIT = 60 << 20


def dot(a, b, ca=1, cb=0):
    return lax.dot_general(a, b, (((ca,), (cb,)), ((), ())), preferred_element_type=F32)


def rows8(value):
    return jnp.sum(value.reshape(value.shape[0] // 8, 8, value.shape[1]), axis=0)


def pick_kernel(send_ref, own_ref, down_ref, up_ref, table, picked):
    table[...] = own_ref[...].astype(F32)
    rim = down_ref.shape[0]
    for n in range(2 * rim):
        row = send_ref[0, n // rim, n % rim]
        picked[pl.ds(n, 1), :] = table[pl.ds(row, 1), :]
    down_ref[...] = picked[pl.ds(0, rim), :].astype(BF16)
    up_ref[...] = picked[pl.ds(rim, rim), :].astype(BF16)


def pick_rows(send_rows, own):
    count = send_rows.size
    return pl.pallas_call(
        pick_kernel,
        in_specs=[
            pl.BlockSpec(memory_space=pltpu.SMEM),
            pl.BlockSpec(memory_space=pltpu.VMEM),
        ],
        out_specs=[pl.BlockSpec(memory_space=pltpu.VMEM)] * 2,
        out_shape=[jax.ShapeDtypeStruct((count // 2, own.shape[1]), BF16)] * 2,
        scratch_shapes=[pltpu.VMEM(own.shape, F32), pltpu.VMEM((count, own.shape[1]), F32)],
        compiler_params=pltpu.CompilerParams(vmem_limit_bytes=VMEM_LIMIT),
        name="pick_rows",
    )(send_rows, own)


def main_kernel(
    idx_new,
    idx_old,
    mask_ref,
    own_ref,
    below_ref,
    above_ref,
    cot_ref,
    w_src,
    w_dst,
    w_msg,
    gain_ref,
    ebias_ref,
    w_self,
    w_agg,
    nbias_ref,
    w_out,
    upd_ref,
    grad_ref,
    back_below_ref,
    back_above_ref,
    packed_ref,
    proj,
    gath,
    hid,
    slope,
    xhat,
    inv,
    prod,
    grad_msg,
    dedge,
    nacc,
    dacc,
    dyc,
    pdst,
    wcen,
    wacc,
    vacc,
    *tables,
):
    step = pl.program_id(0)
    nblocks = pl.num_programs(0) - 1
    nodes, width = own_ref.shape
    rim = below_ref.shape[0]
    degree = idx_new.shape[0]
    ones = jnp.full((width, width), 1.0 / width, BF16)
    chunk = 512

    @pl.when(step == 0)
    def _():
        for src, at in ((own_ref, 0), (below_ref, nodes), (above_ref, nodes + rim)):
            for c in range(0, src.shape[0], chunk):
                proj[pl.ds(at + c, chunk), :] = dot(src[pl.ds(c, chunk), :], w_src[...])
        proj[pl.ds(nodes + 2 * rim, 8), :] = jnp.full((8, width), EMPTY, F32)
        for t in tables:
            t[...] = jnp.zeros_like(t)
        wacc[...] = jnp.zeros_like(wacc)
        vacc[...] = jnp.zeros_like(vacc)
        w = w_msg[...].astype(F32)
        w = w - jnp.mean(w, axis=1, keepdims=True)
        high = w.astype(BF16)
        wcen[pl.ds(0, width), :] = high
        wcen[pl.ds(width, width), :] = (w - high.astype(F32)).astype(BF16)

    half = 64
    piece = 256
    edges = degree * BLOCK

    def gather_row(n):
        gath[pl.ds(n, 1), :] = proj[pl.ds(idx_new[n // BLOCK, n % BLOCK], 1), :]

    def scatter_row(n):
        t = tables[n % CHAINS]
        i = idx_old[n // BLOCK, n % BLOCK]
        t[pl.ds(i, 1), :] = t[pl.ds(i, 1), :] + dedge[pl.ds(n, 1), :]

    def layer():
        at = pl.ds(pl.multiple_of((step - 1) * BLOCK, BLOCK), BLOCK)
        own = own_ref[at, :]
        pdst[...] = dot(own, w_dst[...]) + ebias_ref[...]
        for e in range(0, edges, half):
            a = gath[pl.ds(e, half), :] + pdst[pl.ds(e % BLOCK, half), :]
            s = 0.5 * jnp.tanh(0.5 * a) + 0.5
            h = a * s
            slope[pl.ds(e, half), :] = s + h * (1.0 - s)
            hid[pl.ds(e, half), :] = h.astype(BF16)
        for e in range(0, edges, piece):
            hb = hid[pl.ds(e, piece), :]
            x = dot(jnp.concatenate([hb, hb], axis=1), wcen[...])
            xhat[pl.ds(e, piece), :] = x
            prod[pl.ds(e, piece), :] = (x * x).astype(BF16)
        for e in range(0, edges, piece):
            r = lax.rsqrt(dot(prod[pl.ds(e, piece), :], ones) + 1e-05)
            xh = xhat[pl.ds(e, piece), :] * r
            inv[pl.ds(e, piece), :] = r
            xhat[pl.ds(e, piece), :] = xh
            nacc[...] = jnp.sum(xh.reshape(piece // BLOCK, BLOCK, width), axis=0) + (
                nacc[...] if e else 0.0
            )
        gain = gain_ref[...]
        total = nacc[...]
        sb = (total * gain).astype(BF16)
        pre = dot(own, w_self[...]) + dot(sb, w_agg[...]) + nbias_ref[...]
        row = lax.broadcasted_iota(jnp.int32, (128, 128), 0)
        col = lax.broadcasted_iota(jnp.int32, (128, 128), 1)
        full = jnp.ones((128, 128), BF16)
        mask = []
        for n in range(BLOCK // 128):
            m = mask_ref[n].astype(F32)
            mask.append(dot(jnp.where(row == col, m, 0.0).astype(BF16), full))
        mask = jnp.concatenate(mask, axis=0)
        cot = cot_ref[...]
        dob = (cot * mask).astype(BF16)
        du = dot(dob, w_out[...], 1, 1)
        s = 0.5 * jnp.tanh(0.5 * pre) + 0.5
        u = pre * s
        dpre = du * (s + u * (1.0 - s))
        ub = u.astype(BF16)
        dpb = dpre.astype(BF16)
        ds = dot(dpb, w_agg[...], 1, 1)
        dy = ds * gain
        dyc[...] = dy - jnp.mean(dy, axis=1, keepdims=True)
        upd_ref[...] = (own.astype(F32) + mask * dot(ub, w_out[...])).astype(BF16)
        grad_ref[at, :] = cot + dot(dpb, w_self[...], 1, 1)
        wacc[3] += dot(own, dpb, 0, 0)
        wacc[4] += dot(sb, dpb, 0, 0)
        wacc[5] += dot(ub, dob, 0, 0)
        vacc[0] += rows8(ds * total)
        vacc[2] += rows8(dpre)
        for e in range(0, edges, half):
            xh = xhat[pl.ds(e, half), :]
            prod[pl.ds(e, half), :] = (dyc[pl.ds(e % BLOCK, half), :] * xh).astype(BF16)
        dy = jnp.broadcast_to(dyc[...][None], (piece // BLOCK, BLOCK, width)).reshape(piece, width)
        for e in range(0, edges, piece):
            along = dot(prod[pl.ds(e, piece), :], ones)
            dm = inv[pl.ds(e, piece), :] * (dy - xhat[pl.ds(e, piece), :] * along)
            grad_msg[pl.ds(e, piece), :] = dm.astype(BF16)
        for e in range(0, edges, piece):
            dh = dot(grad_msg[pl.ds(e, piece), :], w_msg[...], 1, 1)
            da = dh * slope[pl.ds(e, piece), :]
            dedge[pl.ds(e, piece), :] = da
            dacc[...] = jnp.sum(da.reshape(piece // BLOCK, BLOCK, width), axis=0) + (
                dacc[...] if e else 0.0
            )
        wacc[2] += dot(hid[...], grad_msg[...], 0, 0)
        d = dacc[...]
        db = d.astype(BF16)
        grad_ref[at, :] += dot(db, w_dst[...], 1, 1)
        wacc[1] += dot(own, db, 0, 0)
        vacc[1] += rows8(d)

    @pl.when(step == 0)
    def _():
        for n in range(edges):
            gather_row(n)

    @pl.when(step > 0)
    def _():
        layer()
        for n in range(edges):
            scatter_row(n)
            gather_row(n)

    @pl.when(step == nblocks)
    def _():
        gsrc = jnp.zeros((width, width), F32)
        for src, at, out_ref in (
            (own_ref, 0, None),
            (below_ref, nodes, back_below_ref),
            (above_ref, nodes + rim, back_above_ref),
        ):
            for c in range(0, src.shape[0], chunk):
                d = tables[0][pl.ds(at + c, chunk), :]
                for t in tables[1:]:
                    d = d + t[pl.ds(at + c, chunk), :]
                db = d.astype(BF16)
                back = dot(db, w_src[...], 1, 1)
                if out_ref is None:
                    grad_ref[pl.ds(c, chunk), :] += back
                else:
                    out_ref[pl.ds(c, chunk), :] = back.astype(BF16)
                gsrc = gsrc + dot(src[pl.ds(c, chunk), :], db, 0, 0)
        wacc[0] = gsrc
        for n in range(6):
            packed_ref[pl.ds(n * width, width), :] = wacc[n].astype(BF16)
        pick = lax.broadcasted_iota(jnp.int32, (16, width), 0)
        tail = jnp.zeros((16, width), F32)
        for n in range(3):
            tail = jnp.where(pick == n, jnp.sum(vacc[n], axis=0, keepdims=True), tail)
        packed_ref[pl.ds(6 * width, 16), :] = tail.astype(BF16)
        rest = packed_ref.shape[0] - 6 * width - 16
        packed_ref[pl.ds(6 * width + 16, rest), :] = jnp.zeros((rest, width), BF16)


def main_call(own, below, above, cotangent, idx, mask, weights):
    nodes, width = own.shape
    rim = below.shape[0]
    degree = idx.shape[0]
    nblocks = nodes // BLOCK
    table = nodes + 2 * rim + 8
    whole = pl.BlockSpec(memory_space=pltpu.VMEM)

    def now(i):
        return jnp.minimum(i, nblocks - 1)

    def held(i):
        return jnp.clip(i - 1, 0, nblocks - 1)


    w_src, w_dst, w_msg, gain, ebias, w_self, w_agg, nbias, w_out = weights
    edges = degree * BLOCK
    fixed = lambda shape: pl.BlockSpec(shape, lambda i: (0,) * len(shape))
    scratch = [
        pltpu.VMEM((table, width), F32),
        pltpu.VMEM((edges, width), F32),
        pltpu.VMEM((edges, width), BF16),
        pltpu.VMEM((edges, width), F32),
        pltpu.VMEM((edges, width), F32),
        pltpu.VMEM((edges, width), F32),
        pltpu.VMEM((edges, width), BF16),
        pltpu.VMEM((edges, width), BF16),
        pltpu.VMEM((edges, width), F32),
        pltpu.VMEM((BLOCK, width), F32),
        pltpu.VMEM((BLOCK, width), F32),
        pltpu.VMEM((BLOCK, width), F32),
        pltpu.VMEM((BLOCK, width), F32),
        pltpu.VMEM((2 * width, width), BF16),
        pltpu.VMEM((6, width, width), F32),
        pltpu.VMEM((3, 8, width), F32),
    ] + [pltpu.VMEM((table, width), F32) for _ in range(CHAINS)]
    return pl.pallas_call(
        main_kernel,
        grid=(nblocks + 1,),
        in_specs=[
            pl.BlockSpec((degree, BLOCK), lambda i: (0, now(i)), memory_space=pltpu.SMEM),
            pl.BlockSpec((degree, BLOCK), lambda i: (0, held(i)), memory_space=pltpu.SMEM),
            pl.BlockSpec((BLOCK // 128, 1, 128), lambda i: (held(i), 0, 0)),
            fixed(own.shape),
            fixed(below.shape),
            fixed(above.shape),
            pl.BlockSpec((BLOCK, width), lambda i: (held(i), 0)),
        ]
        + [fixed((width, width))] * 3
        + [fixed((1, width))] * 2
        + [fixed((width, width))] * 2
        + [fixed((1, width))]
        + [fixed((width, width))],
        out_specs=[
            pl.BlockSpec((BLOCK, width), lambda i: (held(i), 0)),
            fixed((nodes, width)),
            fixed((rim, width)),
            fixed((rim, width)),
            fixed((8 * width, width)),
        ],
        out_shape=[
            jax.ShapeDtypeStruct((nodes, width), BF16),
            jax.ShapeDtypeStruct((nodes, width), F32),
            jax.ShapeDtypeStruct((rim, width), BF16),
            jax.ShapeDtypeStruct((rim, width), BF16),
            jax.ShapeDtypeStruct((8 * width, width), BF16),
        ],
        scratch_shapes=scratch,
        compiler_params=pltpu.CompilerParams(
            dimension_semantics=("arbitrary",), vmem_limit_bytes=VMEM_LIMIT
        ),
        name="main_layer",
    )(
        idx,
        idx,
        mask,
        own,
        below,
        above,
        cotangent,
        w_src,
        w_dst,
        w_msg,
        gain.reshape(1, width),
        ebias.reshape(1, width),
        w_self,
        w_agg,
        nbias.reshape(1, width),
        w_out,
    )


def add_kernel(send_ref, part_ref, first_ref, second_ref, out_ref, back, *tables):
    rim = first_ref.shape[0]
    back[pl.ds(0, rim), :] = first_ref[...].astype(F32)
    back[pl.ds(rim, rim), :] = second_ref[...].astype(F32)
    for t in tables:
        t[...] = jnp.zeros_like(t)
    for n in range(2 * rim):
        t = tables[n % len(tables)]
        at = pl.ds(send_ref[0, n // rim, n % rim], 1)
        t[at, :] = t[at, :] + back[pl.ds(n, 1), :]
    total = part_ref[...]
    for t in tables:
        total = total + t[...]
    out_ref[...] = total


def add_returned(send_rows, part, first, second):
    nodes, width = part.shape
    rim = first.shape[0]
    vmem = pl.BlockSpec(memory_space=pltpu.VMEM)
    return pl.pallas_call(
        add_kernel,
        in_specs=[pl.BlockSpec(memory_space=pltpu.SMEM), vmem, vmem, vmem],
        out_specs=vmem,
        out_shape=jax.ShapeDtypeStruct(part.shape, F32),
        scratch_shapes=[pltpu.VMEM((2 * rim, width), F32)]
        + [pltpu.VMEM((nodes, width), F32) for _ in range(CHAINS)],
        compiler_params=pltpu.CompilerParams(vmem_limit_bytes=VMEM_LIMIT),
        input_output_aliases={1: 0},
        name="add_returned",
    )(send_rows, part, first, second)


def sum_kernel(parts_ref, out_ref):
    total = parts_ref[0].astype(F32)
    for n in range(1, parts_ref.shape[0]):
        total = total + parts_ref[n].astype(F32)
    out_ref[...] = jnp.broadcast_to(total.astype(BF16)[None], out_ref.shape)


def finish_kernel(factor, sums_ref, *outs):
    width = sums_ref.shape[1]
    for n in range(6):
        outs[n][...] = sums_ref[pl.ds(n * width, width), :].astype(F32) * factor
    tail = sums_ref[pl.ds(6 * width, 16), :].astype(F32) * factor
    for n in range(3):
        outs[6 + n][...] = tail[n : n + 1, :]


def weight_sums(packed, factor):
    size = lax.axis_size("tile")
    count, width = packed.shape
    share = count // size
    vmem = pl.BlockSpec(memory_space=pltpu.VMEM)
    parts = lax.all_to_all(packed.reshape(size, share, width), "tile", 0, 0, tiled=True)
    mine = pl.pallas_call(
        sum_kernel,
        in_specs=[vmem],
        out_specs=vmem,
        out_shape=jax.ShapeDtypeStruct((size, share, width), BF16),
        name="sum_parts",
    )(parts)
    sums = lax.all_to_all(mine, "tile", 0, 0, tiled=True).reshape(count, width)
    outs = pl.pallas_call(
        partial(finish_kernel, factor),
        in_specs=[vmem],
        out_specs=[vmem] * 9,
        out_shape=[jax.ShapeDtypeStruct((width, width), F32)] * 6
        + [jax.ShapeDtypeStruct((1, width), F32)] * 3,
        name="finish_weights",
    )(sums)
    return outs[:6], [v.reshape(width) for v in outs[6:]]


def on_device(
    node_latent,
    cotangent,
    neighbours,
    send_rows,
    node_mask,
    w_src,
    w_dst,
    w_msg,
    edge_gain,
    edge_bias,
    w_self,
    w_agg,
    node_bias,
    w_out,
):
    nodes = node_latent.shape[0]
    rim = send_rows.shape[2]
    size = lax.axis_size("tile")
    up = [(i, (i + 1) % size) for i in range(size)]
    down = [(j, i) for i, j in up]
    to_below, to_above = pick_rows(send_rows, node_latent)
    below = lax.ppermute(to_above, "tile", up)
    above = lax.ppermute(to_below, "tile", down)
    idx = jnp.where(neighbours < 0, nodes + 2 * rim, neighbours)
    mask = node_mask.reshape(nodes // 128, 1, 128)
    weights = (w_src, w_dst, w_msg, edge_gain, edge_bias, w_self, w_agg, node_bias, w_out)
    updated, part, back_below, back_above, packed = main_call(
        node_latent, below, above, cotangent, idx, mask, weights
    )
    first = lax.ppermute(back_above, "tile", up)
    second = lax.ppermute(back_below, "tile", down)
    latent_grad = add_returned(send_rows, part, first, second)
    factor = (nodes * size) ** (-0.5)
    mats, vecs = weight_sums(packed, factor)
    g_src, g_dst, g_msg, g_self, g_agg, g_out = mats
    g_gain, g_ebias, g_nbias = vecs
    return (
        updated,
        latent_grad,
        g_src,
        g_dst,
        g_msg,
        g_gain,
        g_ebias,
        g_self,
        g_agg,
        g_nbias,
        g_out,
    )


def solution(mesh):
    tiles = ("scene", "tile")
    in_specs = (
        P(tiles, None),
        P(tiles, None),
        P(None, tiles),
        P(tiles, None, None),
        P(tiles),
    ) + (P(),) * 9
    mat, vec = P("scene", None), P("scene")
    out_specs = (P(tiles, None), P(tiles, None), mat, mat, mat, vec, vec, mat, mat, vec, mat)
    return jax.shard_map(
        on_device, mesh=mesh, in_specs=in_specs, out_specs=out_specs, check_vma=False
    )
```
